32 devices in a mesh: groups: 2 (over y), rows: 4 (over z), tm: 4 (over x, core).
Axes of the slice: x: 2, y: 2, z: 4, core: 2. Of those that a mesh axis runs over, the one named last changes fastest.
Arguments:
- video: bfloat16 [2, 16, 8, 96, 128], P('groups', 'tm', 'rows'), parts along dimension 0, may hold values from -6 to 6
- gamma_first: float32 [96], replicated, may hold values from 0.25 to 1.75
- kernel_first: bfloat16 [96, 2592], replicated, may hold values from -0.125 to 0.125
- bias_first: float32 [96], replicated, may hold values from -3 to 3
- gamma_second: float32 [96], replicated, may hold values from 0.25 to 1.75
- kernel_second: bfloat16 [96, 2592], replicated, may hold values from -0.125 to 0.125
- bias_second: float32 [96], replicated, may hold values from -3 to 3
Outputs:
- encoded: bfloat16 [2, 16, 8, 96, 128], P('groups', 'tm', 'rows'), parts along dimension 0
The draws below stay inside these ranges and needn't reach their ends.
There are 2 independent parts, one for each index of `groups`. The reference program is written for one: setup_inputs(seed, part) draws one part's arguments, and reference() takes and returns one part's arrays. A program takes and returns all parts, laid end to end along the dimension named above; an argument that names none is the same for every part. Nothing has to cross between parts.
All inputs are finite; a program needn't handle non-finite values.
Results may differ from the reference program's by a relative error of at most 0.0036.
Values may be sent and summed in bfloat16 or wider, within the bound.
A program may use at most 64 MiB of HBM per device.

```python
import jax
import jax.numpy as jnp
from jax import lax

C = 96
CLIPS = 1
COLS = 128
FRAMES = 16
HEIGHT = 8


def steps_of(key, shape, split, smallest, largest):
    loudness, own = 1.0, jax.random.fold_in(key, 6)
    for dim, parts in split:
        steps = jnp.exp(jax.random.uniform(jax.random.fold_in(own, dim), (parts,), jnp.float32, smallest / len(split), largest / len(split)))
        loudness = loudness * jnp.repeat(steps, shape[dim] // parts).reshape([-1 if axis == dim else 1 for axis in range(len(shape))])
    return loudness


def normal_values(own_key, shape, scale, reach, pieces=(), kind=jnp.bfloat16):
    level = steps_of(own_key, shape, pieces, -0.22, 0.18) if pieces else 1.0
    entries = jax.random.normal(own_key, shape, jnp.float32) * scale * level
    return jnp.minimum(jnp.maximum(entries, -reach), reach).astype(kind)


def setup_inputs(seed: int = 0, part: int = 0) -> dict:
    seeds = jax.random.split(jax.random.key(seed), 8)
    part_splits = jax.random.split(jax.random.fold_in(seeds[7], part), 8)
    return {
        "video": normal_values(part_splits[0], (CLIPS, FRAMES, HEIGHT, C, COLS), 1.0, 6.0, ((1, 4), (2, 4))),
        "gamma_first": jnp.clip(1.0 + 0.15 * jax.random.normal(seeds[1], (C,), jnp.float32), 0.25, 1.75),
        "kernel_first": normal_values(seeds[2], (C, 27 * C), (27 * C) ** -0.5, 0.125),
        "bias_first": normal_values(seeds[3], (C,), 0.5, 3.0, (), jnp.float32),
        "gamma_second": jnp.clip(1.0 + 0.15 * jax.random.normal(seeds[4], (C,), jnp.float32), 0.25, 1.75),
        "kernel_second": normal_values(seeds[5], (C, 27 * C), (27 * C) ** -0.5, 0.125),
        "bias_second": normal_values(seeds[6], (C,), 0.5, 3.0, (), jnp.float32),
    }


epsilon = 1e-06

def norm_silu(values, gain):
    meansq = lax.optimization_barrier(jnp.mean(values * values, axis=3, keepdims=True))
    scaled = values * lax.rsqrt(meansq + epsilon) * gain[:, None]
    return jax.nn.silu(scaled)

def causal_conv(active, kernel, offset):
    clips, frames, height, chans, width = active.shape
    padded = jnp.pad(active, ((0, 0), (2, 0), (1, 1), (0, 0), (1, 1)))
    taps = kernel.astype(jnp.float32).reshape(chans, 3, 3, 3, chans)

    def one_frame(index):
        window = lax.dynamic_slice_in_dim(padded, index, 3, axis=1).astype(jnp.float32)
        summed = jnp.zeros((clips, height, chans, width), jnp.float32)
        for frame_off in range(3):
            for row_off in range(3):
                for col_off in range(3):
                    piece = window[:, frame_off, row_off:row_off + height, :, col_off:col_off + width]
                    summed = summed + jnp.einsum('oc,bhcw->bhow', taps[:, frame_off, row_off, col_off, :], piece, precision=lax.Precision.HIGHEST)
        return summed
    outputs = lax.map(one_frame, jnp.arange(frames, dtype=jnp.int32))
    return jnp.moveaxis(outputs, 0, 1) + offset[:, None]

def reference(video, gamma_first, kernel_first, bias_first, gamma_second, kernel_second, bias_second):
    first = norm_silu(video.astype(jnp.float32), gamma_first).astype(jnp.bfloat16)
    hidden = causal_conv(first, kernel_first, bias_first)
    second = norm_silu(hidden, gamma_second).astype(jnp.bfloat16)
    result = causal_conv(second, kernel_second, bias_second)
    return (video.astype(jnp.float32) + result).astype(jnp.bfloat16)
```

```python
import jax
import jax.numpy as jnp
from jax import lax
from jax.experimental import pallas as pl
from jax.experimental.pallas import tpu as pltpu
from jax.sharding import PartitionSpec as P

MESH = pl.DeviceIdType.MESH
epsilon = 1e-06


def block_kernel(
    video, k_first, k_second, g_first, b_first, g_second, b_second, out,
    ext, st_a, st_b, w_a, w_b, by_a, by_b, sum_a, sum_b, vecs, small_0, small_1, small_2, small_3, local_sem, send_sem, recv_sem,
):
    frames, rows, chans, width = video.shape[1:]
    group = 9 * chans
    t = lax.axis_index("tm")
    r = lax.axis_index("rows")
    has_prev = t > 0
    has_next = t < lax.axis_size("tm") - 1
    has_up = r > 0
    has_down = r < lax.axis_size("rows") - 1

    def both(one, other):
        return jnp.logical_and(one, other)

    up, down, later = {"rows": r - 1}, {"rows": r + 1}, {"tm": t + 1}

    barrier = pltpu.get_barrier_semaphore()
    for cond, where in ((has_up, up), (has_down, down), (has_prev, {"tm": t - 1})):
        @pl.when(cond)
        def _():
            pl.semaphore_signal(barrier, inc=1, device_id=where, device_id_type=MESH)

    own_rows = slice(2, 2 + rows)
    above, below = slice(0, 2), slice(2 + rows, 4 + rows)
    own = pltpu.make_async_copy(video.at[0], ext.at[frames:, own_rows], local_sem.at[0])
    load_a = pltpu.make_async_copy(k_first, w_a, local_sem.at[1])
    load_b = pltpu.make_async_copy(k_second, w_b, local_sem.at[2])
    own.start()
    small = [
        pltpu.make_async_copy(src, dst, local_sem.at[3 + n])
        for n, (src, dst) in enumerate(
            ((g_first, small_0), (b_first, small_1), (g_second, small_2), (b_second, small_3))
        )
    ]
    for copy in small:
        copy.start()
    load_a.start()
    load_b.start()

    own.wait()
    pl.semaphore_wait(
        barrier, has_up.astype(jnp.int32) + has_down.astype(jnp.int32) + has_next.astype(jnp.int32)
    )

    order = list(range(frames))[::-1]

    def plan(slot, src, dst, where, sends, takes):
        copy = pltpu.make_async_remote_copy(
            src_ref=src, dst_ref=dst, send_sem=send_sem.at[slot], recv_sem=recv_sem.at[slot],
            device_id=where, device_id_type=MESH,
        )
        return copy, sends, takes

    beside, passed = {}, {}
    for f in range(frames):
        mine = ext.at[frames + f, own_rows]
        beside[f] = (
            plan(f, mine, ext.at[frames + f, below], up, has_up, has_down),
            plan(frames + f, mine, ext.at[frames + f, above], down, has_down, has_up),
        )
        passed[f] = (
            plan(2 * frames + f, ext.at[frames + f, below], ext.at[f, below], later,
                 both(has_next, has_down), both(has_prev, has_down)),
            plan(3 * frames + f, ext.at[frames + f, above], ext.at[f, above], later,
                 both(has_next, has_up), both(has_prev, has_up)),
        )
    onward = plan(4 * frames, ext.at[frames:, own_rows], ext.at[0:frames, own_rows], later, has_next, has_prev)

    def start(made):
        for copy, sends, _ in made:
            pl.when(sends)(copy.start)

    def taken(made):
        for copy, _, takes in made:
            pl.when(takes)(copy.wait_recv)

    def sent(made):
        for copy, sends, _ in made:
            pl.when(sends)(copy.wait_send)

    start(beside[order[0]])
    start([onward])
    for f in order[1:]:
        start(beside[f])

    @pl.when(jnp.logical_not(has_up))
    def _():
        ext[:, above] = jnp.zeros((2 * frames, 2, chans, width), jnp.bfloat16)

    @pl.when(jnp.logical_not(has_down))
    def _():
        ext[:, below] = jnp.zeros((2 * frames, 2, chans, width), jnp.bfloat16)

    for n, ref in enumerate((small_0, small_1, small_2, small_3)):
        small[n].wait()
        vecs[n] = jnp.broadcast_to(ref[...], (width, chans)).T

    lane = lax.broadcasted_iota(jnp.int32, (chans, width), 1)

    def act(values, gain):
        meansq = jnp.sum(values * values, axis=0, keepdims=True) * (1.0 / chans)
        half = values * lax.rsqrt(meansq + epsilon) * (gain * 0.5)
        return half + half * jnp.tanh(half)

    def place(stack, f, p, field):
        shifted = [
            jnp.where(lane == 0, 0.0, pltpu.roll(field, 1, 1)).astype(jnp.bfloat16),
            field.astype(jnp.bfloat16),
            jnp.where(lane == width - 1, 0.0, pltpu.roll(field, width - 1, 1)).astype(jnp.bfloat16),
        ]
        for k in range(3):
            at = (p * 3 + k) * chans
            stack[f, at : at + chans, :] = shifted[k]

    def first_at(f, places):
        for p in places:
            place(st_a, f, p, act(ext[f, p].astype(jnp.float32), vecs[0]))

    def split(weights, by_frame):
        for i in range(3):
            by_frame[i * chans : (i + 1) * chans, :] = weights[:, i * group : (i + 1) * group]

    def windows(stack, f, many):
        return jnp.concatenate(
            [stack[f, p * 3 * chans : (p + 3) * 3 * chans, :] for p in range(many)], axis=1
        )

    def taps(by_frame, stack, many, count, f):
        low, high = max(0, f - count + 1), min(2, f)
        total = jnp.dot(
            by_frame[low * chans : (high + 1) * chans, :], windows(stack, f, many),
            preferred_element_type=jnp.float32,
        )
        return {f - i: total[(i - low) * chans : (i - low + 1) * chans] for i in range(low, high + 1)}

    one = jnp.float32(1.0)
    inside_up = jnp.where(has_up, one, 0.0)
    inside_down = jnp.where(has_down, one, 0.0)

    class Path:
        def __init__(self, earlier):
            self.first_left = {
                o: {f for f in range(o, o + 3) if earlier or f >= frames} for o in range(frames + 2)
            }
            self.second_left = {
                o: {f for f in range(o, o + 3) if earlier or f >= 2} for o in range(frames)
            }
            self.begun, self.ready = set(), []

        def first_conv(self, f):
            for o, part in taps(by_a, st_a, rows + 2, frames + 2, f).items():
                if ("a", o) in self.begun:
                    sum_a[o] += part
                else:
                    sum_a[o] = part
                    self.begun.add(("a", o))
                self.first_left[o].discard(f)
                if not self.first_left[o]:
                    self.ready.append(o)

        def second_act(self, o):
            for row in range(rows + 2):
                value = act(sum_a[o, :, row * width : (row + 1) * width] + vecs[1], vecs[2])
                if row == 0:
                    value = value * inside_up
                if row == rows + 1:
                    value = value * inside_down
                place(st_b, o, row, value)

        def second_conv(self, f):
            for o, part in taps(by_b, st_b, rows, frames, f).items():
                if ("b", o) in self.begun:
                    part = sum_b[o] + part
                self.begun.add(("b", o))
                self.second_left[o].discard(f)
                if self.second_left[o]:
                    sum_b[o] = part
                    continue
                for row in range(rows):
                    value = part[:, row * width : (row + 1) * width] + vecs[3]
                    out[0, o, row] = (ext[frames + o, row + 2].astype(jnp.float32) + value).astype(jnp.bfloat16)

        def finish(self):
            ready, self.ready = self.ready, []
            for o in ready:
                self.second_act(o)
                self.second_conv(o)

    middle = range(2, 2 + rows)
    edges = [0, 1, 2 + rows, 3 + rows]
    for f in order:
        first_at(frames + f, middle)
    load_a.wait()
    split(w_a, by_a)
    load_b.wait()
    split(w_b, by_b)

    def own_frame(path, f, extra=()):
        taken(beside[f])
        start(passed[f])
        first_at(frames + f, edges)
        for e in extra:
            first_at(e, middle)
        ready, path.ready = path.ready, []
        path.first_conv(frames + f)
        for o in ready:
            path.second_act(o)
            path.second_conv(o)

    def earlier_frame(path, f):
        taken(passed[f])
        first_at(f, edges)
        ready, path.ready = path.ready, []
        path.first_conv(f)
        for o in ready:
            path.second_act(o)
            path.second_conv(o)

    @pl.when(jnp.logical_not(has_prev))
    def _():
        path = Path(False)
        for f in order:
            own_frame(path, f)
        path.finish()

    @pl.when(has_prev)
    def _():
        path = Path(True)
        onward[0].wait_recv()
        for f in order:
            own_frame(path, f, (f,))
        for f in order:
            earlier_frame(path, f)
        path.finish()

    for f in order:
        sent(beside[f])
        sent(passed[f])
    sent([onward])


def local(video, gamma_first, kernel_first, bias_first, gamma_second, kernel_second, bias_second):
    frames, rows, chans, width = video.shape[1:]
    ext = pltpu.VMEM((2 * frames, rows + 4, chans, width), jnp.bfloat16)
    wide = pltpu.VMEM((2 * frames, (rows + 4) * 3 * chans, width), jnp.bfloat16)
    stack = pltpu.VMEM((frames + 2, (rows + 2) * 3 * chans, width), jnp.bfloat16)
    weights = pltpu.VMEM(kernel_first.shape, jnp.bfloat16)
    by_frame = pltpu.VMEM((3 * chans, 9 * chans), jnp.bfloat16)
    vmem = pl.BlockSpec(memory_space=pltpu.VMEM)
    hbm = pl.BlockSpec(memory_space=pl.ANY)
    return pl.pallas_call(
        block_kernel,
        out_shape=pltpu.VMEM(video.shape, jnp.bfloat16),
        in_specs=[hbm] * 7,
        out_specs=vmem,
        scratch_shapes=[
            ext, wide, stack, weights, weights, by_frame, by_frame,
            pltpu.VMEM((frames + 2, chans, (rows + 2) * width), jnp.float32),
            pltpu.VMEM((frames, chans, rows * width), jnp.float32),
            pltpu.VMEM((4, chans, width), jnp.float32),
            *[pltpu.VMEM((1, chans), jnp.float32)] * 4,
            pltpu.SemaphoreType.DMA((7,)),
            pltpu.SemaphoreType.DMA((4 * frames + 1,)),
            pltpu.SemaphoreType.DMA((4 * frames + 1,)),
        ],
        compiler_params=pltpu.CompilerParams(collective_id=0, has_side_effects=True),
        name="residual_block",
    )(
        video, kernel_first, kernel_second, gamma_first[None, :], bias_first[None, :],
        gamma_second[None, :], bias_second[None, :],
    )


def solution(mesh):
    in_specs = (P("groups", "tm", "rows", None, None), P(), P(), P(), P(), P(), P())
    out_specs = P("groups", "tm", "rows", None, None)
    return jax.shard_map(local, mesh=mesh, in_specs=in_specs, out_specs=out_specs, check_vma=False)
```

```python
import jax
import jax.numpy as jnp
from jax import lax
from jax.experimental import pallas as pl
from jax.experimental.pallas import tpu as pltpu
from jax.sharding import PartitionSpec as P

MESH = pl.DeviceIdType.MESH
epsilon = 1e-06


def block_kernel(
    video, k_first, k_second, g_first, b_first, g_second, b_second, out,
    ext, st_a, st_b, w_a, w_b, by_a, by_b, sum_a, sum_b, vecs, small_0, small_1, small_2, small_3, local_sem, send_sem, recv_sem,
):
    frames, rows, chans, width = video.shape[1:]
    group = 9 * chans
    t = lax.axis_index("tm")
    r = lax.axis_index("rows")
    has_prev = t > 0
    has_next = t < lax.axis_size("tm") - 1
    has_up = r > 0
    has_down = r < lax.axis_size("rows") - 1

    def both(one, other):
        return jnp.logical_and(one, other)

    up, down, later = {"rows": r - 1}, {"rows": r + 1}, {"tm": t + 1}

    barrier = pltpu.get_barrier_semaphore()
    for cond, where in ((has_up, up), (has_down, down), (has_prev, {"tm": t - 1})):
        @pl.when(cond)
        def _():
            pl.semaphore_signal(barrier, inc=1, device_id=where, device_id_type=MESH)

    own_rows = slice(2, 2 + rows)
    above, below = slice(0, 2), slice(2 + rows, 4 + rows)
    own = pltpu.make_async_copy(video.at[0], ext.at[frames:, own_rows], local_sem.at[0])
    load_a = pltpu.make_async_copy(k_first, w_a, local_sem.at[1])
    load_b = pltpu.make_async_copy(k_second, w_b, local_sem.at[2])
    own.start()
    small = [
        pltpu.make_async_copy(src, dst, local_sem.at[3 + n])
        for n, (src, dst) in enumerate(
            ((g_first, small_0), (b_first, small_1), (g_second, small_2), (b_second, small_3))
        )
    ]
    for copy in small:
        copy.start()
    load_a.start()
    load_b.start()

    own.wait()
    pl.semaphore_wait(
        barrier, has_up.astype(jnp.int32) + has_down.astype(jnp.int32) + has_next.astype(jnp.int32)
    )

    order = list(range(frames))[::-1]

    def plan(slot, src, dst, where, sends, takes):
        copy = pltpu.make_async_remote_copy(
            src_ref=src, dst_ref=dst, send_sem=send_sem.at[slot], recv_sem=recv_sem.at[slot],
            device_id=where, device_id_type=MESH,
        )
        return copy, sends, takes

    beside, passed = {}, {}
    for f in range(frames):
        mine = ext.at[frames + f, own_rows]
        beside[f] = (
            plan(f, mine, ext.at[frames + f, below], up, has_up, has_down),
            plan(frames + f, mine, ext.at[frames + f, above], down, has_down, has_up),
        )
        passed[f] = (
            plan(2 * frames + f, ext.at[frames + f, below], ext.at[f, below], later,
                 both(has_next, has_down), both(has_prev, has_down)),
            plan(3 * frames + f, ext.at[frames + f, above], ext.at[f, above], later,
                 both(has_next, has_up), both(has_prev, has_up)),
        )
    onward = plan(4 * frames, ext.at[frames:, own_rows], ext.at[0:frames, own_rows], later, has_next, has_prev)

    def start(made):
        for copy, sends, _ in made:
            pl.when(sends)(copy.start)

    def taken(made):
        for copy, _, takes in made:
            pl.when(takes)(copy.wait_recv)

    def sent(made):
        for copy, sends, _ in made:
            pl.when(sends)(copy.wait_send)

    start(beside[order[0]])
    start([onward])
    for f in order[1:]:
        start(beside[f])

    @pl.when(jnp.logical_not(has_up))
    def _():
        ext[:, above] = jnp.zeros((2 * frames, 2, chans, width), jnp.bfloat16)

    @pl.when(jnp.logical_not(has_down))
    def _():
        ext[:, below] = jnp.zeros((2 * frames, 2, chans, width), jnp.bfloat16)

    for n, ref in enumerate((small_0, small_1, small_2, small_3)):
        small[n].wait()
        vecs[n] = jnp.broadcast_to(ref[...] * (0.5 if n % 2 == 0 else 1.0), (width, chans)).T

    lane = lax.broadcasted_iota(jnp.int32, (chans, width), 1)

    def act(values, half_gain, keep=None):
        meansq = jnp.sum(values * values, axis=0, keepdims=True) * (1.0 / chans)
        factor = lax.rsqrt(meansq + epsilon)
        half = values * (factor if keep is None else factor * keep) * half_gain
        return half + half * jnp.tanh(half)

    def place(stack, f, p, field):
        shifted = [
            jnp.where(lane == 0, 0.0, pltpu.roll(field, 1, 1)).astype(jnp.bfloat16),
            field.astype(jnp.bfloat16),
            jnp.where(lane == width - 1, 0.0, pltpu.roll(field, width - 1, 1)).astype(jnp.bfloat16),
        ]
        for k in range(3):
            at = (p * 3 + k) * chans
            stack[f, at : at + chans, :] = shifted[k]

    def first_at(f, places):
        for p in places:
            place(st_a, f, p, act(ext[f, p].astype(jnp.float32), vecs[0]))

    def split(weights, by_frame):
        for i in range(3):
            by_frame[i * chans : (i + 1) * chans, :] = weights[:, i * group : (i + 1) * group]

    def taps(by_frame, stack, many, count, f, pieces):
        low, high = max(0, f - count + 1), min(2, f)
        total = None
        for begin, end in pieces:
            window = jnp.concatenate(
                [stack[f, p * 3 * chans + begin : p * 3 * chans + end, :] for p in range(many)], axis=1
            )
            part = jnp.dot(
                by_frame[low * chans : (high + 1) * chans, begin:end], window,
                preferred_element_type=jnp.float32,
            )
            total = part if total is None else total + part
        return {f - i: total[(i - low) * chans : (i - low + 1) * chans] for i in range(low, high + 1)}

    one = jnp.float32(1.0)
    inside_up = jnp.where(has_up, one, 0.0)
    inside_down = jnp.where(has_down, one, 0.0)

    class Path:
        def __init__(self, earlier):
            self.first_left = {
                o: {f for f in range(o, o + 3) if earlier or f >= frames} for o in range(frames + 2)
            }
            self.second_left = {
                o: {f for f in range(o, o + 3) if earlier or f >= 2} for o in range(frames)
            }
            self.begun, self.multiply, self.ready, self.placed = set(), [], [], []

        def first_conv(self, f):
            for o, part in taps(by_a, st_a, rows + 2, frames + 2, f, ((0, group),)).items():
                if ("a", o) in self.begun:
                    sum_a[o] += part
                else:
                    sum_a[o] = part
                    self.begun.add(("a", o))
                self.first_left[o].discard(f)
                if not self.first_left[o]:
                    self.ready.append(o)

        def second_act(self, o):
            for row in range(rows + 2):
                keep = {0: inside_up, rows + 1: inside_down}.get(row)
                value = act(sum_a[o, :, row * width : (row + 1) * width] + vecs[1], vecs[2], keep)
                place(st_b, o, row, value)

        def second_conv(self, f):
            for o, part in taps(by_b, st_b, rows, frames, f, ((0, 512), (512, group))).items():
                if ("b", o) in self.begun:
                    part = sum_b[o] + part
                self.begun.add(("b", o))
                self.second_left[o].discard(f)
                if self.second_left[o]:
                    sum_b[o] = part
                    continue
                for row in range(rows):
                    value = part[:, row * width : (row + 1) * width] + vecs[3]
                    out[0, o, row] = (ext[frames + o, row + 2].astype(jnp.float32) + value).astype(jnp.bfloat16)

        def advance(self, arrived=(), extra=(), now=False):
            multiply, self.multiply = self.multiply, []
            ready, self.ready = self.ready, []
            placed, self.placed = self.placed, []
            for f in multiply:
                self.first_conv(f)
            for o in placed:
                self.second_conv(o)
            for f in arrived:
                first_at(f, edges)
                if now:
                    self.first_conv(f)
                else:
                    self.multiply.append(f)
            for o in ready:
                self.second_act(o)
                self.placed.append(o)
            for f in extra:
                first_at(f, middle)

        def finish(self):
            while self.multiply or self.ready or self.placed:
                self.advance()

    middle = range(2, 2 + rows)
    edges = [0, 1, 2 + rows, 3 + rows]
    for f in order:
        first_at(frames + f, middle)
    load_a.wait()
    split(w_a, by_a)
    load_b.wait()
    split(w_b, by_b)

    def own_frame(path, f, extra=(), now=True):
        taken(beside[f])
        start(passed[f])
        path.advance((frames + f,), extra, now)

    def earlier_frame(path, f, now=True):
        taken(passed[f])
        path.advance((f,), (), now)

    @pl.when(jnp.logical_not(has_prev))
    def _():
        path = Path(False)
        for f in order:
            own_frame(path, f)
        path.finish()

    @pl.when(has_prev)
    def _():
        path = Path(True)
        onward[0].wait_recv()
        for f in order:
            own_frame(path, f, (f,), f > 0)
        for f in order:
            earlier_frame(path, f, f < 2)
        path.finish()

    for f in order:
        sent(beside[f])
        sent(passed[f])
    sent([onward])


def local(video, gamma_first, kernel_first, bias_first, gamma_second, kernel_second, bias_second):
    frames, rows, chans, width = video.shape[1:]
    ext = pltpu.VMEM((2 * frames, rows + 4, chans, width), jnp.bfloat16)
    wide = pltpu.VMEM((2 * frames, (rows + 4) * 3 * chans, width), jnp.bfloat16)
    stack = pltpu.VMEM((frames + 2, (rows + 2) * 3 * chans, width), jnp.bfloat16)
    weights = pltpu.VMEM(kernel_first.shape, jnp.bfloat16)
    by_frame = pltpu.VMEM((3 * chans, 9 * chans), jnp.bfloat16)
    vmem = pl.BlockSpec(memory_space=pltpu.VMEM)
    hbm = pl.BlockSpec(memory_space=pl.ANY)
    return pl.pallas_call(
        block_kernel,
        out_shape=pltpu.VMEM(video.shape, jnp.bfloat16),
        in_specs=[hbm] * 7,
        out_specs=vmem,
        scratch_shapes=[
            ext, wide, stack, weights, weights, by_frame, by_frame,
            pltpu.VMEM((frames + 2, chans, (rows + 2) * width), jnp.float32),
            pltpu.VMEM((frames, chans, rows * width), jnp.float32),
            pltpu.VMEM((4, chans, width), jnp.float32),
            *[pltpu.VMEM((1, chans), jnp.float32)] * 4,
            pltpu.SemaphoreType.DMA((7,)),
            pltpu.SemaphoreType.DMA((4 * frames + 1,)),
            pltpu.SemaphoreType.DMA((4 * frames + 1,)),
        ],
        compiler_params=pltpu.CompilerParams(collective_id=0, has_side_effects=True),
        name="residual_block",
    )(
        video, kernel_first, kernel_second, gamma_first[None, :], bias_first[None, :],
        gamma_second[None, :], bias_second[None, :],
    )


def solution(mesh):
    in_specs = (P("groups", "tm", "rows", None, None), P(), P(), P(), P(), P(), P())
    out_specs = P("groups", "tm", "rows", None, None)
    return jax.shard_map(local, mesh=mesh, in_specs=in_specs, out_specs=out_specs, check_vma=False)
```

```python
import jax
import jax.numpy as jnp
from jax import lax
from jax.experimental import pallas as pl
from jax.experimental.pallas import tpu as pltpu
from jax.sharding import PartitionSpec as P

MESH = pl.DeviceIdType.MESH
epsilon = 1e-06


def block_kernel(
    video, k_first, k_second, g_first, b_first, g_second, b_second, out,
    ext, st_a, st_b, w_a, w_b, by_a, by_b, sum_a, sum_b, vecs, small_0, small_1, small_2, small_3, local_sem, send_sem, recv_sem,
):
    frames, rows, chans, width = video.shape[1:]
    group = 9 * chans
    t = lax.axis_index("tm")
    r = lax.axis_index("rows")
    has_prev = t > 0
    has_next = t < lax.axis_size("tm") - 1
    has_up = r > 0
    has_down = r < lax.axis_size("rows") - 1

    up, down, later = {"rows": r - 1}, {"rows": r + 1}, {"tm": t + 1}

    barrier = pltpu.get_barrier_semaphore()
    for cond, where in ((has_up, up), (has_down, down), (has_prev, {"tm": t - 1})):
        @pl.when(cond)
        def _():
            pl.semaphore_signal(barrier, inc=1, device_id=where, device_id_type=MESH)

    above, below, around, own_rows = slice(0, 2), slice(2, 4), slice(0, 4), slice(4, 4 + rows)
    held_at = [0, 1, *range(4, 4 + rows), 2, 3]
    own = pltpu.make_async_copy(video.at[0], ext.at[frames:, own_rows], local_sem.at[0])
    load_a = pltpu.make_async_copy(k_first, w_a, local_sem.at[1])
    load_b = pltpu.make_async_copy(k_second, w_b, local_sem.at[2])
    own.start()
    small = [
        pltpu.make_async_copy(src, dst, local_sem.at[3 + n])
        for n, (src, dst) in enumerate(
            ((g_first, small_0), (b_first, small_1), (g_second, small_2), (b_second, small_3))
        )
    ]
    for copy in small:
        copy.start()

    own.wait()
    pl.semaphore_wait(
        barrier, has_up.astype(jnp.int32) + has_down.astype(jnp.int32) + has_next.astype(jnp.int32)
    )

    order = list(range(frames))[::-1]

    def plan(slot, src, dst, where, sends, takes):
        copy = pltpu.make_async_remote_copy(
            src_ref=src, dst_ref=dst, send_sem=send_sem.at[slot], recv_sem=recv_sem.at[slot],
            device_id=where, device_id_type=MESH,
        )
        return copy, sends, takes

    beside, passed = {}, {}
    for f in range(frames):
        mine = ext.at[frames + f, own_rows]
        beside[f] = (
            plan(f, mine, ext.at[frames + f, below], up, has_up, has_down),
            plan(frames + f, mine, ext.at[frames + f, above], down, has_down, has_up),
        )
        passed[f] = (
            plan(2 * frames + f, ext.at[frames + f, around], ext.at[f, around], later, has_next, has_prev),
        )
    onward = plan(3 * frames, ext.at[frames:, own_rows], ext.at[0:frames, own_rows], later, has_next, has_prev)

    def start(made):
        for copy, sends, _ in made:
            pl.when(sends)(copy.start)

    def taken(made):
        for copy, _, takes in made:
            pl.when(takes)(copy.wait_recv)

    def sent(made):
        for copy, sends, _ in made:
            pl.when(sends)(copy.wait_send)

    start(beside[order[0]])
    start([onward])
    for f in order[1:]:
        start(beside[f])

    load_a.start()
    load_b.start()

    @pl.when(jnp.logical_not(has_up))
    def _():
        ext[frames:, above] = jnp.zeros((frames, 2, chans, width), jnp.bfloat16)

    @pl.when(jnp.logical_not(has_down))
    def _():
        ext[frames:, below] = jnp.zeros((frames, 2, chans, width), jnp.bfloat16)

    for n, ref in enumerate((small_0, small_1, small_2, small_3)):
        small[n].wait()
        vecs[n] = jnp.broadcast_to(ref[...] * (0.5 if n % 2 == 0 else 1.0), (width, chans)).T

    lane = lax.broadcasted_iota(jnp.int32, (chans, width), 1)

    def act(values, half_gain, keep=None):
        meansq = jnp.sum(values * values, axis=0, keepdims=True) * (1.0 / chans)
        factor = lax.rsqrt(meansq + epsilon)
        half = values * (factor if keep is None else factor * keep) * half_gain
        return half + half * jnp.tanh(half)

    def place(stack, f, p, field):
        shifted = [
            jnp.where(lane == 0, 0.0, pltpu.roll(field, 1, 1)).astype(jnp.bfloat16),
            field.astype(jnp.bfloat16),
            jnp.where(lane == width - 1, 0.0, pltpu.roll(field, width - 1, 1)).astype(jnp.bfloat16),
        ]
        for k in range(3):
            at = (p * 3 + k) * chans
            stack[f, at : at + chans, :] = shifted[k]

    def first_at(f, places):
        for p in places:
            place(st_a, f, p, act(ext[f, held_at[p]].astype(jnp.float32), vecs[0]))

    def split(weights, by_frame):
        for i in range(3):
            by_frame[i * chans : (i + 1) * chans, :] = weights[:, i * group : (i + 1) * group]

    def taps(by_frame, stack, many, count, f, pieces):
        low, high = max(0, f - count + 1), min(2, f)
        total = None
        for begin, end in pieces:
            window = jnp.concatenate(
                [stack[f, p * 3 * chans + begin : p * 3 * chans + end, :] for p in range(many)], axis=1
            )
            part = jnp.dot(
                by_frame[low * chans : (high + 1) * chans, begin:end], window,
                preferred_element_type=jnp.float32,
            )
            total = part if total is None else total + part
        return {f - i: total[(i - low) * chans : (i - low + 1) * chans] for i in range(low, high + 1)}

    one = jnp.float32(1.0)
    inside_up = jnp.where(has_up, one, 0.0)
    inside_down = jnp.where(has_down, one, 0.0)

    class Path:
        def __init__(self, earlier):
            self.first_left = {
                o: {f for f in range(o, o + 3) if earlier or f >= frames} for o in range(frames + 2)
            }
            self.second_left = {
                o: {f for f in range(o, o + 3) if earlier or f >= 2} for o in range(frames)
            }
            self.begun, self.multiply, self.ready, self.placed = set(), [], [], []

        def first_conv(self, f):
            for o, part in taps(by_a, st_a, rows + 2, frames + 2, f, ((0, group),)).items():
                if ("a", o) in self.begun:
                    sum_a[o] += part
                else:
                    sum_a[o] = part
                    self.begun.add(("a", o))
                self.first_left[o].discard(f)
                if not self.first_left[o]:
                    self.ready.append(o)

        def second_act(self, o):
            for row in range(rows + 2):
                keep = {0: inside_up, rows + 1: inside_down}.get(row)
                value = act(sum_a[o, :, row * width : (row + 1) * width] + vecs[1], vecs[2], keep)
                place(st_b, o, row, value)

        def second_conv(self, f):
            for o, part in taps(by_b, st_b, rows, frames, f, ((0, 512), (512, group))).items():
                if ("b", o) in self.begun:
                    part = sum_b[o] + part
                self.begun.add(("b", o))
                self.second_left[o].discard(f)
                if self.second_left[o]:
                    sum_b[o] = part
                    continue
                for row in range(rows):
                    value = part[:, row * width : (row + 1) * width] + vecs[3]
                    out[0, o, row] = (ext[frames + o, held_at[row + 2]].astype(jnp.float32) + value).astype(jnp.bfloat16)

        def advance(self, arrived=(), extra=(), now=False):
            multiply, self.multiply = self.multiply, []
            ready, self.ready = self.ready, []
            placed, self.placed = self.placed, []
            for f in multiply:
                self.first_conv(f)
            for o in placed:
                self.second_conv(o)
            for f in arrived:
                first_at(f, edges)
                if now:
                    self.first_conv(f)
                else:
                    self.multiply.append(f)
            for o in ready:
                self.second_act(o)
                self.placed.append(o)
            for f in extra:
                first_at(f, middle)

        def finish(self):
            while self.multiply or self.ready or self.placed:
                self.advance()

    middle = range(2, 2 + rows)
    edges = [0, 1, 2 + rows, 3 + rows]
    for f in order:
        first_at(frames + f, middle)
    load_a.wait()
    split(w_a, by_a)
    load_b.wait()
    split(w_b, by_b)

    def own_frame(path, f, extra=(), now=True):
        taken(beside[f])
        start(passed[f])
        path.advance((frames + f,), extra, now)

    def earlier_frame(path, f, now=True):
        taken(passed[f])
        path.advance((f,), (), now)

    @pl.when(jnp.logical_not(has_prev))
    def _():
        path = Path(False)
        for f in order:
            own_frame(path, f)
        path.finish()

    @pl.when(has_prev)
    def _():
        path = Path(True)
        onward[0].wait_recv()
        for f in order:
            own_frame(path, f, (f,), f > 0)
        for f in order:
            earlier_frame(path, f, f < 2)
        path.finish()

    for f in order:
        sent(beside[f])
        sent(passed[f])
    sent([onward])


def local(video, gamma_first, kernel_first, bias_first, gamma_second, kernel_second, bias_second):
    frames, rows, chans, width = video.shape[1:]
    ext = pltpu.VMEM((2 * frames, rows + 4, chans, width), jnp.bfloat16)
    wide = pltpu.VMEM((2 * frames, (rows + 4) * 3 * chans, width), jnp.bfloat16)
    stack = pltpu.VMEM((frames + 2, (rows + 2) * 3 * chans, width), jnp.bfloat16)
    weights = pltpu.VMEM(kernel_first.shape, jnp.bfloat16)
    by_frame = pltpu.VMEM((3 * chans, 9 * chans), jnp.bfloat16)
    vmem = pl.BlockSpec(memory_space=pltpu.VMEM)
    hbm = pl.BlockSpec(memory_space=pl.ANY)
    return pl.pallas_call(
        block_kernel,
        out_shape=pltpu.VMEM(video.shape, jnp.bfloat16),
        in_specs=[hbm] * 7,
        out_specs=vmem,
        scratch_shapes=[
            ext, wide, stack, weights, weights, by_frame, by_frame,
            pltpu.VMEM((frames + 2, chans, (rows + 2) * width), jnp.float32),
            pltpu.VMEM((frames, chans, rows * width), jnp.float32),
            pltpu.VMEM((4, chans, width), jnp.float32),
            *[pltpu.VMEM((1, chans), jnp.float32)] * 4,
            pltpu.SemaphoreType.DMA((7,)),
            pltpu.SemaphoreType.DMA((3 * frames + 1,)),
            pltpu.SemaphoreType.DMA((3 * frames + 1,)),
        ],
        compiler_params=pltpu.CompilerParams(collective_id=0, has_side_effects=True),
        name="residual_block",
    )(
        video, kernel_first, kernel_second, gamma_first[None, :], bias_first[None, :],
        gamma_second[None, :], bias_second[None, :],
    )


def solution(mesh):
    in_specs = (P("groups", "tm", "rows", None, None), P(), P(), P(), P(), P(), P())
    out_specs = P("groups", "tm", "rows", None, None)
    return jax.shard_map(local, mesh=mesh, in_specs=in_specs, out_specs=out_specs, check_vma=False)
```
